32 devices in a mesh: img: 4 (over z), tile: 8 (over y, x, core).
Axes of the slice: x: 2, y: 2, z: 4, core: 2. Of those that a mesh axis runs over, the one named last changes fastest.
Arguments:
- features: bfloat16 [64, 2400, 256], P(('img', 'tile')), may hold values from -6 to 6
- cluster_ids: int32 [64, 4, 2400], P(('img', 'tile')), may hold values from 0 to 63
- soft_weights: bfloat16 [64, 4, 2400], P(('img', 'tile')), may hold values from 0.019897461 to 1
- counts: int32 [64], P(('img', 'tile')), may hold values from 600 to 2400, as said below
- centroids: bfloat16 [64, 256], replicated, may hold values from -3 to 3
- covariance: float32 [16384, 16384], P('img', 'tile'), may hold values from -1.5 to 1.5
Outputs:
- updated: float32 [16384, 16384], P('img', 'tile')
The draws below stay inside these ranges and needn't reach their ends.
Inputs may be any that keep to these rules, and one draw needn't show every extreme that they name: `counts`: some image has exactly 2400 valid features and some exactly 600.
All inputs are finite; a program needn't handle non-finite values.
Results may differ from the reference program's by a relative error of at most 0.0003.
Values sent between devices are 32-bit elements; how exact they have to be, the bound alone decides.
No kernel may reach another device: no remote copies, remote signals or barrier semaphores. Data moves between devices by JAX's collectives and lax.ppermute only.
A program may use at most 128 MiB of HBM per device.

```python
import math
import jax
import jax.numpy as jnp
from jax import lax

CLUSTERS = 64
DESC = 256
TOPK = 4
MAXF = 2400
FMIN = 600
IMAGES = 64
VLAD_DIM = 16384


def draw_counts(key, part):
    first_key, second_key, third_key = jax.random.split(key, 3)
    values = jax.random.randint(first_key, (IMAGES,), FMIN, MAXF + 1, dtype=jnp.int32)
    top_at = jax.random.randint(second_key, (), 0, IMAGES, dtype=jnp.int32)
    low_at = (top_at + 1 + jax.random.randint(third_key, (), 0, IMAGES - 1, dtype=jnp.int32)) % IMAGES
    values = values.at[top_at].set(MAXF)
    values = values.at[low_at].set(FMIN)
    return values


def place_ends(result, stream_key, smallest, largest):
    longest = result.shape.index(max(result.shape))
    spots = []
    for shift in (0, 1):
        where = [jax.random.randint(jax.random.fold_in(stream_key, axis), (), 0, length) for axis, length in enumerate(result.shape)]
        where[longest] = (where[longest] + shift) % result.shape[longest]
        spots.append(tuple(where))
    return result.at[spots[0]].set(smallest).at[spots[1]].set(largest)


def block_levels(own_key, shape, shards, smallest, top_value):
    factor_of, own = 1.0, jax.random.fold_in(own_key, 6)
    for dim, parts in shards:
        heights = jnp.exp(jax.random.uniform(jax.random.fold_in(own, dim), (parts,), jnp.float32, smallest / len(shards), top_value / len(shards)))
        factor_of = factor_of * jnp.repeat(heights, shape[dim] // parts).reshape([-1 if axis == dim else 1 for axis in range(len(shape))])
    return factor_of


def normal_values(stream_key, extent, scale, limit, cuts=(), kind=jnp.bfloat16):
    level = block_levels(stream_key, extent, cuts, -0.22, 0.18) if cuts else 1.0
    entries = jax.random.normal(stream_key, extent, jnp.float32) * scale * level
    return jnp.minimum(jnp.maximum(entries, -limit), limit).astype(kind)


def setup_inputs(seed: int = 0) -> dict:
    keys = jax.random.split(jax.random.key(seed), 7)
    features = normal_values(keys[0], (IMAGES, MAXF, DESC), 1.0, 6.0, ((0, 32),))
    cluster_ids = place_ends(jax.random.randint(keys[1], (IMAGES, TOPK, MAXF), 0, CLUSTERS), jax.random.fold_in(keys[1], 1), 0, CLUSTERS - 1).astype(jnp.int32)
    soft_weights = jnp.clip(jnp.exp(math.log(1.0) - 3.9171631 * jax.random.uniform(keys[2], (IMAGES, TOPK, MAXF), jnp.float32) ** block_levels(keys[2], (IMAGES, TOPK, MAXF), ((0, 32),), -0.2, 0.2)), 0.019897461, 1.0).astype(jnp.bfloat16)
    counts = draw_counts(jax.random.fold_in(keys[6], 71), 0)
    centroids = normal_values(keys[4], (CLUSTERS, DESC), 0.5, 3.0)
    covariance = normal_values(keys[5], (VLAD_DIM, VLAD_DIM), 0.1, 1.5, ((0, 4), (1, 8)), jnp.float32)
    return {"features": features, "cluster_ids": cluster_ids, "soft_weights": soft_weights, "counts": counts, "centroids": centroids, "covariance": covariance}


def aggregate(feature_rows, id_rows, weight_rows, feature_count, centroids):
    position = jnp.arange(MAXF)
    in_range = position < feature_count
    labels = jnp.arange(CLUSTERS)
    assign = jnp.zeros((CLUSTERS, MAXF), jnp.float32)
    for slot in range(TOPK):
        matched = id_rows[slot][None, :] == labels[:, None]
        assign = assign + jnp.where(matched, weight_rows[slot].astype(jnp.float32)[None, :], jnp.float32(0.0))
    assign = jnp.where(in_range[None, :], assign, jnp.float32(0.0)).astype(jnp.bfloat16)
    weight_sum = lax.optimization_barrier(jnp.sum(assign.astype(jnp.float32), axis=1))
    residual = jnp.dot(assign, feature_rows, preferred_element_type=jnp.float32)
    residual = residual - weight_sum[:, None] * centroids.astype(jnp.float32)
    magnitude = jnp.sqrt(lax.optimization_barrier(jnp.sum(residual * residual, axis=1, keepdims=True)) + 1e-06)
    return (residual / magnitude).reshape(-1)

def reference(features, cluster_ids, soft_weights, counts, centroids, covariance):

    def one_image(packed):
        return aggregate(packed[0], packed[1], packed[2], packed[3], centroids)
    vlad_rows = lax.map(one_image, (features, cluster_ids, soft_weights, counts))
    outer_sum = jnp.dot(vlad_rows.T, vlad_rows, precision=lax.Precision.HIGHEST)
    factor = float(DESC) / float(IMAGES)
    return covariance + factor * outer_sum
```

```python
import functools

import jax
import jax.numpy as jnp
from jax import lax
from jax.experimental import pallas as pl
from jax.experimental.pallas import tpu as pltpu
from jax.sharding import PartitionSpec as P

VMEM = pltpu.VMEM
BF16 = jnp.bfloat16
F32 = jnp.float32


def aggregate_kernel(counts, ids, weights, centroids, features, rows):
    image = pl.program_id(0)
    top, slots = ids.shape[1:]
    clusters = centroids.shape[0]
    position = lax.broadcasted_iota(jnp.int32, (top, slots), 1)
    valid_ids = jnp.where(position < counts[image], ids[0], -1)
    values = weights[0].astype(F32)
    labels = lax.broadcasted_iota(jnp.int32, (clusters, slots), 0)
    assign = jnp.zeros((clusters, slots), F32)
    for slot in range(top):
        matched = valid_ids[slot : slot + 1] == labels
        assign = assign + jnp.where(matched, values[slot : slot + 1], 0.0)
    assign = assign.astype(BF16)
    weight_sum = jnp.sum(assign.astype(F32), axis=1, keepdims=True)
    residual = jnp.dot(assign, features[0], preferred_element_type=F32)
    residual = residual - weight_sum * centroids[...].astype(F32)
    square = jnp.sum(residual * residual, axis=1, keepdims=True)
    rows[0] = residual / jnp.sqrt(square + 1e-06)


def aggregate(features, cluster_ids, soft_weights, counts, centroids):
    images, slots, width = features.shape
    top = cluster_ids.shape[1]
    clusters = centroids.shape[0]
    return pl.pallas_call(
        aggregate_kernel,
        grid=(images,),
        in_specs=[
            pl.BlockSpec(memory_space=pltpu.SMEM),
            pl.BlockSpec((1, top, slots), lambda i: (i, 0, 0)),
            pl.BlockSpec((1, top, slots), lambda i: (i, 0, 0)),
            pl.BlockSpec((clusters, width), lambda i: (0, 0)),
            pl.BlockSpec((1, slots, width), lambda i: (i, 0, 0)),
        ],
        out_specs=pl.BlockSpec((1, clusters, width), lambda i: (i, 0, 0)),
        out_shape=jax.ShapeDtypeStruct((images, clusters, width), F32),
        compiler_params=pltpu.CompilerParams(vmem_limit_bytes=16 << 20),
        name="aggregate",
    )(counts, cluster_ids, soft_weights, centroids, features)


def pack_kernel(peers, block, own, other, *parts):
    core = lax.rem(lax.axis_index("tile"), 2)
    me = jnp.where(core == 0, lax.axis_index("img"), lax.axis_index("tile") // 2)
    images = own.shape[0]
    for step in range(peers):
        start = pl.multiple_of(lax.bitwise_xor(me, step) * block, block)
        parts[step][pl.ds(core * images, images)] = own[:, pl.ds(start, block)]
        parts[step][pl.ds((1 - core) * images, images)] = other[:, pl.ds(start, block)]


def pack(own, other, peers, block):
    images, _, width = own.shape
    return pl.pallas_call(
        functools.partial(pack_kernel, peers, block),
        in_specs=[pl.BlockSpec(memory_space=VMEM)] * 2,
        out_specs=[pl.BlockSpec(memory_space=VMEM)] * peers,
        out_shape=[jax.ShapeDtypeStruct((2 * images, block, width), F32)] * peers,
        compiler_params=pltpu.CompilerParams(vmem_limit_bytes=4 << 20),
        name="pack",
    )(own, other)


def load_kernel(block, source, target, sems):
    steps = source.shape[0] // block
    copies = [
        pltpu.make_async_copy(
            source.at[pl.ds(i * block, block)], target.at[pl.ds(i * block, block)], sems.at[i]
        )
        for i in range(steps)
    ]
    for copy in copies:
        copy.start()
    for copy in copies:
        copy.wait()


def load(covariance, block):
    rows, cols = covariance.shape
    size = rows * cols * 4
    return pl.pallas_call(
        functools.partial(load_kernel, block),
        in_specs=[pl.BlockSpec(memory_space=pl.ANY)],
        out_specs=pl.BlockSpec(memory_space=VMEM),
        out_shape=VMEM((rows, cols), F32),
        scratch_shapes=[pltpu.SemaphoreType.DMA((rows // block,))],
        compiler_params=pltpu.CompilerParams(vmem_limit_bytes=1 << 20),
        cost_estimate=pl.CostEstimate(flops=0, bytes_accessed=size, transcendentals=0),
        name="load",
    )(covariance)


def split(value):
    high = value.astype(BF16)
    low = (value - high.astype(F32)).astype(BF16)
    return high, low


def update_kernel(peers, factor, stages, *refs):
    mine, theirs = refs[:peers], refs[peers : 2 * peers]
    covariance, updated, left, right, stage, sems = refs[2 * peers :]
    core = lax.rem(lax.axis_index("tile"), 2)
    group, block, width = mine[0].shape
    part = group // peers
    count = group * peers
    half = block // 2

    def prepare(row_refs, col_refs, base):
        for k in range(half):
            pieces = []
            for j in range(peers):
                for t in range(peers):
                    pieces.append(col_refs[t][j * part : (j + 1) * part, base + k, :])
            high, low = split(jnp.concatenate(pieces, axis=0) * factor)
            columns = slice(k * width, (k + 1) * width)
            right[0 * count : 1 * count, columns] = high
            right[1 * count : 2 * count, columns] = low
            right[2 * count : 3 * count, columns] = high
        for k in range(block):
            pieces = [row_refs[j][:, k, :] for j in range(peers)]
            high, low = split(jnp.concatenate(pieces, axis=0))
            left[k, 0 * count : 1 * count] = high
            left[k, 1 * count : 2 * count] = high
            left[k, 2 * count : 3 * count] = low

    @pl.when(core == 0)
    def _():
        prepare(mine, theirs, 0)

    @pl.when(core == 1)
    def _():
        prepare(theirs, mine, half)

    def copy_out(step, slot):
        start = pl.multiple_of(step * width, width)
        return pltpu.make_async_copy(stage.at[slot], updated.at[pl.ds(start, width)], sems.at[slot])

    def row_step(step, carry):
        slot = lax.rem(step, stages)

        @pl.when(step >= stages)
        def _():
            copy_out(step - stages, slot).wait()

        product = lax.dot_general(
            left[step], right[...], (((0,), (0,)), ((), ())), preferred_element_type=F32
        )
        start = pl.multiple_of(step * width, width)
        stage[slot] = covariance[pl.ds(start, width)] + product
        copy_out(step, slot).start()
        return carry

    lax.fori_loop(0, block, row_step, 0)
    for step in range(max(block - stages, 0), block):
        copy_out(step, step % stages).wait()


def update(mine, theirs, covariance, factor):
    peers = len(mine)
    group, block, width = mine[0].shape
    count = group * peers
    rows, cols = covariance.shape
    stages = 3
    return pl.pallas_call(
        functools.partial(update_kernel, peers, factor, stages),
        in_specs=[pl.BlockSpec(memory_space=VMEM)] * (2 * peers + 1),
        out_specs=pl.BlockSpec(memory_space=pl.ANY),
        out_shape=jax.ShapeDtypeStruct((rows, cols), F32),
        scratch_shapes=[
            VMEM((block, 3 * count, width), BF16),
            VMEM((3 * count, cols), BF16),
            VMEM((stages, width, cols), F32),
            pltpu.SemaphoreType.DMA((stages,)),
        ],
        compiler_params=pltpu.CompilerParams(vmem_limit_bytes=12 << 20),
        name="update",
    )(*mine, *theirs, covariance)


def body(features, cluster_ids, soft_weights, counts, centroids, covariance):
    peers = lax.axis_size("img")
    tiles = lax.axis_size("tile")
    clusters, width = centroids.shape
    images = features.shape[0]
    block = clusters // peers
    factor = float(width) / float(images * peers * tiles)

    def device(img, group, core):
        return (img * (tiles // 2) + group) * 2 + core

    everyone = [(i, g, c) for i in range(peers) for g in range(tiles // 2) for c in range(2)]

    def send(value, target):
        pairs = [(device(*d), device(*target(*d))) for d in everyone]
        return lax.ppermute(value, ("img", "tile"), pairs)

    def to_other(value):
        return send(value, lambda i, g, c: (i, g, 1 - c))

    def first(value, k):
        return send(value, lambda i, g, c: (i ^ k, g, c) if c == 0 else (i, g ^ k, c))

    def second(value, k):
        return send(value, lambda i, g, c: (i, g ^ k, c) if c == 0 else (i ^ k, g, c))

    own = aggregate(features, cluster_ids, soft_weights, counts, centroids)
    other = to_other(own)
    parts = pack(own, other, peers, block)
    received = [parts[0]]
    for k in range(1, peers):
        received.append(first(parts[k], k))
    gathered = jnp.concatenate(received, axis=0)
    mine = [gathered]
    for k in range(1, peers):
        mine.append(second(gathered, k))
    theirs = []
    for k in range(peers):
        theirs.append(to_other(mine[k]))
    held = load(covariance, 2 * width)
    return update(mine, theirs, held, factor)


def solution(mesh):
    return jax.shard_map(
        body,
        mesh=mesh,
        in_specs=(
            P(("img", "tile"), None, None),
            P(("img", "tile"), None, None),
            P(("img", "tile"), None, None),
            P(("img", "tile")),
            P(),
            P("img", "tile"),
        ),
        out_specs=P("img", "tile"),
        check_vma=False,
    )
```

```python
import functools

import jax
import jax.numpy as jnp
from jax import lax
from jax.experimental import pallas as pl
from jax.experimental.pallas import tpu as pltpu
from jax.sharding import PartitionSpec as P

VMEM = pltpu.VMEM
BF16 = jnp.bfloat16
F32 = jnp.float32


def aggregate_kernel(counts, ids_in, weights_in, centroids_in, features_in, rows, *scratch):
    ids, weights, centroids, features, sems = scratch
    images, top, slots = ids.shape
    clusters = centroids.shape[0]
    small = [
        pltpu.make_async_copy(source, target, sems.at[n])
        for n, (source, target) in enumerate(
            [(ids_in, ids), (weights_in, weights), (centroids_in, centroids)]
        )
    ]
    large = [
        pltpu.make_async_copy(features_in.at[n], features.at[n], sems.at[len(small) + n])
        for n in range(images)
    ]
    for copy in small + large:
        copy.start()
    for copy in small:
        copy.wait()
    labels = lax.broadcasted_iota(jnp.int32, (clusters, slots), 0)
    position = lax.broadcasted_iota(jnp.int32, (top, slots), 1)
    for image in range(images):
        valid_ids = jnp.where(position < counts[image], ids[image], -1)
        values = weights[image].astype(F32)
        assign = jnp.zeros((clusters, slots), F32)
        for slot in range(top):
            matched = valid_ids[slot : slot + 1] == labels
            assign = assign + jnp.where(matched, values[slot : slot + 1], 0.0)
        assign = assign.astype(BF16)
        weight_sum = jnp.sum(assign.astype(F32), axis=1, keepdims=True)
        large[image].wait()
        residual = jnp.dot(assign, features[image], preferred_element_type=F32)
        residual = residual - weight_sum * centroids[...].astype(F32)
        square = jnp.sum(residual * residual, axis=1, keepdims=True)
        rows[image] = residual / jnp.sqrt(square + 1e-06)


def aggregate(features, cluster_ids, soft_weights, counts, centroids):
    images, _, width = features.shape
    clusters = centroids.shape[0]
    return pl.pallas_call(
        aggregate_kernel,
        in_specs=[pl.BlockSpec(memory_space=pltpu.SMEM)]
        + [pl.BlockSpec(memory_space=pltpu.HBM)] * 4,
        out_specs=pl.BlockSpec(memory_space=VMEM),
        out_shape=VMEM((images, clusters, width), F32),
        scratch_shapes=[
            VMEM(cluster_ids.shape, cluster_ids.dtype),
            VMEM(soft_weights.shape, soft_weights.dtype),
            VMEM(centroids.shape, centroids.dtype),
            VMEM(features.shape, features.dtype),
            pltpu.SemaphoreType.DMA((3 + images,)),
        ],
        compiler_params=pltpu.CompilerParams(vmem_limit_bytes=64000000),
        name="aggregate",
    )(counts, cluster_ids, soft_weights, centroids, features)


def pack_kernel(peers, block, own, other, *parts):
    core = lax.rem(lax.axis_index("tile"), 2)
    me = jnp.where(core == 0, lax.axis_index("img"), lax.axis_index("tile") // 2)
    images = own.shape[0]
    for step in range(peers):
        start = pl.multiple_of(lax.bitwise_xor(me, step) * block, block)
        parts[step][pl.ds(core * images, images)] = own[:, pl.ds(start, block)]
        parts[step][pl.ds((1 - core) * images, images)] = other[:, pl.ds(start, block)]


def pack(own, other, peers, block):
    images, _, width = own.shape
    return pl.pallas_call(
        functools.partial(pack_kernel, peers, block),
        in_specs=[pl.BlockSpec(memory_space=VMEM)] * 2,
        out_specs=[pl.BlockSpec(memory_space=VMEM)] * peers,
        out_shape=[jax.ShapeDtypeStruct((2 * images, block, width), F32)] * peers,
        compiler_params=pltpu.CompilerParams(vmem_limit_bytes=4 << 20),
        cost_estimate=pl.CostEstimate(flops=10**11, bytes_accessed=10**9, transcendentals=0),
        name="pack",
    )(own, other)


def split(value):
    high = value.astype(BF16)
    low = (value - high.astype(F32)).astype(BF16)
    return high, low


def update_kernel(peers, factor, stages, *refs):
    mine, theirs = refs[:peers], refs[peers : 2 * peers]
    covariance, updated, left, right, stage, sems = refs[2 * peers :]
    core = lax.rem(lax.axis_index("tile"), 2)
    group, block, width = mine[0].shape
    part = group // peers
    count = group * peers
    half = block // 2

    def prepare(row_refs, col_refs, base):
        for k in range(half):
            pieces = []
            for j in range(peers):
                for t in range(peers):
                    pieces.append(col_refs[t][j * part : (j + 1) * part, base + k, :])
            high, low = split(jnp.concatenate(pieces, axis=0) * factor)
            columns = slice(k * width, (k + 1) * width)
            right[0 * count : 1 * count, columns] = high
            right[1 * count : 2 * count, columns] = low
            right[2 * count : 3 * count, columns] = high
        for k in range(block):
            pieces = [row_refs[j][:, k, :] for j in range(peers)]
            high, low = split(jnp.concatenate(pieces, axis=0))
            left[k, 0 * count : 1 * count] = high
            left[k, 1 * count : 2 * count] = high
            left[k, 2 * count : 3 * count] = low

    @pl.when(core == 0)
    def _():
        prepare(mine, theirs, 0)

    @pl.when(core == 1)
    def _():
        prepare(theirs, mine, half)

    def copy_out(step, slot):
        start = pl.multiple_of(step * width, width)
        return pltpu.make_async_copy(stage.at[slot], updated.at[pl.ds(start, width)], sems.at[slot])

    def row_step(step, carry):
        slot = lax.rem(step, stages)

        @pl.when(step >= stages)
        def _():
            copy_out(step - stages, slot).wait()

        product = lax.dot_general(
            left[step], right[...], (((0,), (0,)), ((), ())), preferred_element_type=F32
        )
        start = pl.multiple_of(step * width, width)
        stage[slot] = covariance[pl.ds(start, width)] + product
        copy_out(step, slot).start()
        return carry

    lax.fori_loop(0, block, row_step, 0)
    for step in range(max(block - stages, 0), block):
        copy_out(step, step % stages).wait()


def update(mine, theirs, covariance, factor):
    peers = len(mine)
    group, block, width = mine[0].shape
    count = group * peers
    rows, cols = covariance.shape
    stages = 3
    return pl.pallas_call(
        functools.partial(update_kernel, peers, factor, stages),
        in_specs=[pl.BlockSpec(memory_space=VMEM)] * (2 * peers + 1),
        out_specs=pl.BlockSpec(memory_space=pl.ANY),
        out_shape=jax.ShapeDtypeStruct((rows, cols), F32),
        scratch_shapes=[
            VMEM((block, 3 * count, width), BF16),
            VMEM((3 * count, cols), BF16),
            VMEM((stages, width, cols), F32),
            pltpu.SemaphoreType.DMA((stages,)),
        ],
        compiler_params=pltpu.CompilerParams(vmem_limit_bytes=12 << 20),
        name="update",
    )(*mine, *theirs, covariance)


def body(features, cluster_ids, soft_weights, counts, centroids, covariance):
    peers = lax.axis_size("img")
    tiles = lax.axis_size("tile")
    clusters, width = centroids.shape
    images = features.shape[0]
    block = clusters // peers
    factor = float(width) / float(images * peers * tiles)

    def device(img, group, core):
        return (img * (tiles // 2) + group) * 2 + core

    everyone = [(i, g, c) for i in range(peers) for g in range(tiles // 2) for c in range(2)]

    def send(value, target):
        pairs = [(device(*d), device(*target(*d))) for d in everyone]
        return lax.ppermute(value, ("img", "tile"), pairs)

    def to_other(value):
        return send(value, lambda i, g, c: (i, g, 1 - c))

    def first(value, k):
        return send(value, lambda i, g, c: (i ^ k, g, c) if c == 0 else (i, g ^ k, c))

    def second(value, k):
        return send(value, lambda i, g, c: (i, g ^ k, c) if c == 0 else (i ^ k, g, c))

    own = aggregate(features, cluster_ids, soft_weights, counts, centroids)
    other = to_other(own)
    parts = pack(own, other, peers, block)
    received = [parts[0]]
    for k in range(1, peers):
        received.append(first(parts[k], k))
    gathered = jnp.concatenate(received, axis=0)
    mine = [gathered]
    for k in range(1, peers):
        if k % 2 and k > 1:
            mine.append(second(mine[k - 1], 1))
        else:
            mine.append(second(gathered, k))
    theirs = []
    for k in range(peers):
        theirs.append(to_other(mine[k]))
    return update(mine, theirs, covariance, factor)


def solution(mesh):
    return jax.shard_map(
        body,
        mesh=mesh,
        in_specs=(
            P(("img", "tile"), None, None),
            P(("img", "tile"), None, None),
            P(("img", "tile"), None, None),
            P(("img", "tile")),
            P(),
            P("img", "tile"),
        ),
        out_specs=P("img", "tile"),
        check_vma=False,
    )
```

```python
import functools

import jax
import jax.numpy as jnp
from jax import lax
from jax.experimental import pallas as pl
from jax.experimental.pallas import tpu as pltpu
from jax.sharding import PartitionSpec as P

VMEM = pltpu.VMEM
BF16 = jnp.bfloat16
F32 = jnp.float32


def aggregate_kernel(counts_in, ids_in, weights_in, centroids_in, features_in, rows, *scratch):
    counts, ids, weights, centroids, features, sems = scratch
    images, top, slots = ids.shape
    clusters = centroids.shape[0]
    small = [
        pltpu.make_async_copy(source, target, sems.at[n])
        for n, (source, target) in enumerate(
            [
                (counts_in, counts),
                (ids_in, ids),
                (weights_in, weights),
                (centroids_in, centroids),
            ]
        )
    ]
    large = [
        pltpu.make_async_copy(features_in.at[n], features.at[n], sems.at[len(small) + n])
        for n in range(images)
    ]
    for copy in small + large:
        copy.start()
    for copy in small:
        copy.wait()
    labels = lax.broadcasted_iota(jnp.int32, (clusters, slots), 0)
    position = lax.broadcasted_iota(jnp.int32, (top, slots), 1)
    for image in range(images):
        valid_ids = jnp.where(position < counts[image], ids[image], -1)
        values = weights[image].astype(F32)
        assign = jnp.zeros((clusters, slots), F32)
        for slot in range(top):
            matched = valid_ids[slot : slot + 1] == labels
            assign = assign + jnp.where(matched, values[slot : slot + 1], 0.0)
        assign = assign.astype(BF16)
        weight_sum = jnp.sum(assign.astype(F32), axis=1, keepdims=True)
        large[image].wait()
        residual = jnp.dot(assign, features[image], preferred_element_type=F32)
        residual = residual - weight_sum * centroids[...].astype(F32)
        square = jnp.sum(residual * residual, axis=1, keepdims=True)
        rows[image] = residual / jnp.sqrt(square + 1e-06)


def aggregate(features, cluster_ids, soft_weights, counts, centroids):
    images, _, width = features.shape
    clusters = centroids.shape[0]
    return pl.pallas_call(
        aggregate_kernel,
        in_specs=[pl.BlockSpec(memory_space=pltpu.HBM)] * 5,
        out_specs=pl.BlockSpec(memory_space=VMEM),
        out_shape=VMEM((images, clusters, width), F32),
        scratch_shapes=[
            pltpu.SMEM(counts.shape, counts.dtype),
            VMEM(cluster_ids.shape, cluster_ids.dtype),
            VMEM(soft_weights.shape, soft_weights.dtype),
            VMEM(centroids.shape, centroids.dtype),
            VMEM(features.shape, features.dtype),
            pltpu.SemaphoreType.DMA((4 + images,)),
        ],
        compiler_params=pltpu.CompilerParams(vmem_limit_bytes=64000000),
        name="aggregate",
    )(counts, cluster_ids, soft_weights, centroids, features)


def pack_kernel(peers, block, own, other, *parts):
    core = lax.rem(lax.axis_index("tile"), 2)
    me = jnp.where(core == 0, lax.axis_index("img"), lax.axis_index("tile") // 2)
    images = own.shape[0]
    for step in range(peers):
        start = pl.multiple_of(lax.bitwise_xor(me, step) * block, block)
        parts[step][pl.ds(core * images, images)] = own[:, pl.ds(start, block)]
        parts[step][pl.ds((1 - core) * images, images)] = other[:, pl.ds(start, block)]


def pack(own, other, peers, block):
    images, _, width = own.shape
    return pl.pallas_call(
        functools.partial(pack_kernel, peers, block),
        in_specs=[pl.BlockSpec(memory_space=VMEM)] * 2,
        out_specs=[pl.BlockSpec(memory_space=VMEM)] * peers,
        out_shape=[jax.ShapeDtypeStruct((2 * images, block, width), F32)] * peers,
        compiler_params=pltpu.CompilerParams(vmem_limit_bytes=4 << 20),
        cost_estimate=pl.CostEstimate(flops=10**11, bytes_accessed=10**9, transcendentals=0),
        name="pack",
    )(own, other)


def split(value):
    high = value.astype(BF16)
    low = (value - high.astype(F32)).astype(BF16)
    return high, low


def update_kernel(peers, factor, stages, sizes, *refs):
    tree = [refs[sum(sizes[:n]) : sum(sizes[: n + 1])] for n in range(2 * peers)]
    mine, theirs = tree[:peers], tree[peers:]
    covariance, updated, left, right, stage, sems = refs[sum(sizes) :]
    core = lax.rem(lax.axis_index("tile"), 2)
    group = sum(ref.shape[0] for ref in mine[0])
    block, width = mine[0][0].shape[1:]
    part = group // peers
    count = group * peers
    half = block // 2

    def take(pieces, slot, cluster):
        size = pieces[0].shape[0]
        start = slot * part
        return pieces[start // size][start % size : start % size + part, cluster, :]

    def prepare(row_refs, col_refs, base):
        slots = [(j, t) for j in range(peers) for t in range(peers)]
        for k in range(half):
            pieces = [take(col_refs[t], j, base + k) for j, t in slots]
            high, low = split(jnp.concatenate(pieces, axis=0) * factor)
            columns = slice(k * width, (k + 1) * width)
            right[0 * count : 1 * count, columns] = high
            right[1 * count : 2 * count, columns] = low
            right[2 * count : 3 * count, columns] = high
        for k in range(block):
            pieces = [ref[:, k, :] for refs_of in row_refs for ref in refs_of]
            high, low = split(jnp.concatenate(pieces, axis=0))
            left[k, 0 * count : 1 * count] = high
            left[k, 1 * count : 2 * count] = high
            left[k, 2 * count : 3 * count] = low

    @pl.when(core == 0)
    def _():
        prepare(mine, theirs, 0)

    @pl.when(core == 1)
    def _():
        prepare(theirs, mine, half)

    def copy_out(step, slot):
        start = pl.multiple_of(step * width, width)
        return pltpu.make_async_copy(stage.at[slot], updated.at[pl.ds(start, width)], sems.at[slot])

    def row_step(step, carry):
        slot = lax.rem(step, stages)

        @pl.when(step >= stages)
        def _():
            copy_out(step - stages, slot).wait()

        product = lax.dot_general(
            left[step], right[...], (((0,), (0,)), ((), ())), preferred_element_type=F32
        )
        start = pl.multiple_of(step * width, width)
        stage[slot] = covariance[pl.ds(start, width)] + product
        copy_out(step, slot).start()
        return carry

    lax.fori_loop(0, block, row_step, 0)
    for step in range(max(block - stages, 0), block):
        copy_out(step, step % stages).wait()


def update(mine, theirs, covariance, factor):
    peers = len(mine)
    sizes = [len(pieces) for pieces in mine + theirs]
    flat = [piece for pieces in mine + theirs for piece in pieces]
    block, width = flat[0].shape[1:]
    count = sum(piece.shape[0] for pieces in mine for piece in pieces)
    rows, cols = covariance.shape
    stages = 3
    return pl.pallas_call(
        functools.partial(update_kernel, peers, factor, stages, sizes),
        in_specs=[pl.BlockSpec(memory_space=VMEM)] * (len(flat) + 1),
        out_specs=pl.BlockSpec(memory_space=pl.ANY),
        out_shape=jax.ShapeDtypeStruct((rows, cols), F32),
        scratch_shapes=[
            VMEM((block, 3 * count, width), BF16),
            VMEM((3 * count, cols), BF16),
            VMEM((stages, width, cols), F32),
            pltpu.SemaphoreType.DMA((stages,)),
        ],
        compiler_params=pltpu.CompilerParams(vmem_limit_bytes=12 << 20),
        name="update",
    )(*flat, covariance)


def body(features, cluster_ids, soft_weights, counts, centroids, covariance):
    peers = lax.axis_size("img")
    tiles = lax.axis_size("tile")
    clusters, width = centroids.shape
    images = features.shape[0]
    block = clusters // peers
    factor = float(width) / float(images * peers * tiles)

    def device(img, group, core):
        return (img * (tiles // 2) + group) * 2 + core

    everyone = [(i, g, c) for i in range(peers) for g in range(tiles // 2) for c in range(2)]

    def send(value, target):
        pairs = [(device(*d), device(*target(*d))) for d in everyone]
        return lax.ppermute(value, ("img", "tile"), pairs)

    def to_other(value):
        return send(value, lambda i, g, c: (i, g, 1 - c))

    def first(value, k):
        return send(value, lambda i, g, c: (i ^ k, g, c) if c == 0 else (i, g ^ k, c))

    def second(value, k):
        return send(value, lambda i, g, c: (i, g ^ k, c) if c == 0 else (i ^ k, g, c))

    own = aggregate(features, cluster_ids, soft_weights, counts, centroids)
    other = to_other(own)
    parts = pack(own, other, peers, block)
    received = [parts[0]]
    for k in range(1, peers):
        received.append(first(parts[k], k))
    middle = peers // 2
    gathered = [jnp.concatenate(received[:middle]), jnp.concatenate(received[middle:])]
    mine = [gathered]
    for k in range(1, peers):
        low = k & -k
        arrived = []
        for piece in mine[k - low]:
            arrived.append(second(piece, low))
        mine.append(arrived)
    theirs = []
    for k in range(peers):
        pieces = mine[k] if k == peers - 1 else [jnp.concatenate(mine[k])]
        theirs.append([to_other(piece) for piece in pieces])
    return update(mine, theirs, covariance, factor)


def solution(mesh):
    return jax.shard_map(
        body,
        mesh=mesh,
        in_specs=(
            P(("img", "tile"), None, None),
            P(("img", "tile"), None, None),
            P(("img", "tile"), None, None),
            P(("img", "tile")),
            P(),
            P("img", "tile"),
        ),
        out_specs=P("img", "tile"),
        check_vma=False,
    )
```

```python
import functools

import jax
import jax.numpy as jnp
from jax import lax
from jax.experimental import pallas as pl
from jax.experimental.pallas import tpu as pltpu
from jax.sharding import PartitionSpec as P

VMEM = pltpu.VMEM
BF16 = jnp.bfloat16
F32 = jnp.float32


def aggregate_kernel(counts_in, ids_in, weights_in, centroids_in, features_in, rows, *scratch):
    counts, ids, weights, centroids, features, sems = scratch
    images, top, slots = ids.shape
    clusters = centroids.shape[0]
    small = [
        pltpu.make_async_copy(source, target, sems.at[n])
        for n, (source, target) in enumerate(
            [
                (counts_in, counts),
                (ids_in, ids),
                (weights_in, weights),
                (centroids_in, centroids),
            ]
        )
    ]
    large = [
        pltpu.make_async_copy(features_in.at[n], features.at[n], sems.at[len(small) + n])
        for n in range(images)
    ]
    for copy in small + large:
        copy.start()
    for copy in small:
        copy.wait()
    labels = lax.broadcasted_iota(jnp.int32, (clusters, slots), 0)
    position = lax.broadcasted_iota(jnp.int32, (top, slots), 1)
    assigned = []
    for image in range(images):
        valid_ids = jnp.where(position < counts[image], ids[image], -1)
        values = weights[image].astype(F32)
        assign = jnp.zeros((clusters, slots), F32)
        for slot in range(top):
            matched = valid_ids[slot : slot + 1] == labels
            assign = assign + jnp.where(matched, values[slot : slot + 1], 0.0)
        assign = assign.astype(BF16)
        weight_sum = jnp.sum(assign.astype(F32), axis=1, keepdims=True)
        assigned.append((assign, weight_sum * centroids[...].astype(F32)))
    for copy in large:
        copy.wait()
    for image, (assign, offset) in enumerate(assigned):
        residual = jnp.dot(assign, features[image], preferred_element_type=F32) - offset
        square = jnp.sum(residual * residual, axis=1, keepdims=True)
        rows[image] = residual / jnp.sqrt(square + 1e-06)


def aggregate(features, cluster_ids, soft_weights, counts, centroids):
    images, _, width = features.shape
    clusters = centroids.shape[0]
    return pl.pallas_call(
        aggregate_kernel,
        in_specs=[pl.BlockSpec(memory_space=pltpu.HBM)] * 5,
        out_specs=pl.BlockSpec(memory_space=VMEM),
        out_shape=VMEM((images, clusters, width), F32),
        scratch_shapes=[
            pltpu.SMEM(counts.shape, counts.dtype),
            VMEM(cluster_ids.shape, cluster_ids.dtype),
            VMEM(soft_weights.shape, soft_weights.dtype),
            VMEM(centroids.shape, centroids.dtype),
            VMEM(features.shape, features.dtype),
            pltpu.SemaphoreType.DMA((4 + images,)),
        ],
        compiler_params=pltpu.CompilerParams(vmem_limit_bytes=64000000),
        name="aggregate",
    )(counts, cluster_ids, soft_weights, centroids, features)


def pack_kernel(peers, block, own, other, *parts):
    core = lax.rem(lax.axis_index("tile"), 2)
    me = jnp.where(core == 0, lax.axis_index("img"), lax.axis_index("tile") // 2)
    images = own.shape[0]
    for step in range(peers):
        start = pl.multiple_of(lax.bitwise_xor(me, step) * block, block)
        parts[step][pl.ds(core * images, images)] = own[:, pl.ds(start, block)]
        parts[step][pl.ds((1 - core) * images, images)] = other[:, pl.ds(start, block)]


def pack(own, other, peers, block):
    images, _, width = own.shape
    return pl.pallas_call(
        functools.partial(pack_kernel, peers, block),
        in_specs=[pl.BlockSpec(memory_space=VMEM)] * 2,
        out_specs=[pl.BlockSpec(memory_space=VMEM)] * peers,
        out_shape=[jax.ShapeDtypeStruct((2 * images, block, width), F32)] * peers,
        compiler_params=pltpu.CompilerParams(vmem_limit_bytes=4 << 20),
        cost_estimate=pl.CostEstimate(flops=10**11, bytes_accessed=10**9, transcendentals=0),
        name="pack",
    )(own, other)


def split(value):
    high = value.astype(BF16)
    low = (value - high.astype(F32)).astype(BF16)
    return high, low


def update_kernel(peers, factor, stages, sizes, *refs):
    tree = [refs[sum(sizes[:n]) : sum(sizes[: n + 1])] for n in range(2 * peers)]
    mine, theirs = tree[:peers], tree[peers:]
    covariance, updated, left, right, stage, sems = refs[sum(sizes) :]
    core = lax.rem(lax.axis_index("tile"), 2)
    group = sum(ref.shape[0] for ref in mine[0])
    block, width = mine[0][0].shape[1:]
    part = group // peers
    count = group * peers
    half = block // 2

    def take(pieces, slot, cluster):
        size = pieces[0].shape[0]
        start = slot * part
        return pieces[start // size][start % size : start % size + part, cluster, :]

    def prepare_columns(col_refs, base):
        slots = [(j, t) for j in range(peers) for t in range(peers)]
        for k in range(half):
            pieces = [take(col_refs[t], j, base + k) for j, t in slots]
            high, low = split(jnp.concatenate(pieces, axis=0) * factor)
            columns = slice(k * width, (k + 1) * width)
            right[0 * count : 1 * count, columns] = high
            right[1 * count : 2 * count, columns] = low
            right[2 * count : 3 * count, columns] = high

    def prepare_rows(row_refs, clusters):
        for k in clusters:
            pieces = [ref[:, k, :] for refs_of in row_refs for ref in refs_of]
            high, low = split(jnp.concatenate(pieces, axis=0))
            left[k, 0 * count : 1 * count] = high
            left[k, 1 * count : 2 * count] = high
            left[k, 2 * count : 3 * count] = low

    lead = min(stages, block)

    @pl.when(core == 0)
    def _():
        prepare_columns(theirs, 0)
        prepare_rows(mine, range(lead))

    @pl.when(core == 1)
    def _():
        prepare_columns(mine, half)
        prepare_rows(theirs, range(lead))

    def copy_out(step, slot):
        start = pl.multiple_of(step * width, width)
        return pltpu.make_async_copy(stage.at[slot], updated.at[pl.ds(start, width)], sems.at[slot])

    def row_step(step, carry):
        slot = lax.rem(step, stages)

        @pl.when(step >= stages)
        def _():
            copy_out(step - stages, slot).wait()

        product = lax.dot_general(
            left[step], right[...], (((0,), (0,)), ((), ())), preferred_element_type=F32
        )
        start = pl.multiple_of(step * width, width)
        stage[slot] = covariance[pl.ds(start, width)] + product
        copy_out(step, slot).start()
        return carry

    lax.fori_loop(0, lead, row_step, 0)

    @pl.when(core == 0)
    def _():
        prepare_rows(mine, range(lead, block))

    @pl.when(core == 1)
    def _():
        prepare_rows(theirs, range(lead, block))

    lax.fori_loop(lead, block, row_step, 0)
    for step in range(max(block - stages, 0), block):
        copy_out(step, step % stages).wait()


def update(mine, theirs, covariance, factor):
    peers = len(mine)
    sizes = [len(pieces) for pieces in mine + theirs]
    flat = [piece for pieces in mine + theirs for piece in pieces]
    block, width = flat[0].shape[1:]
    count = sum(piece.shape[0] for pieces in mine for piece in pieces)
    rows, cols = covariance.shape
    stages = 3
    return pl.pallas_call(
        functools.partial(update_kernel, peers, factor, stages, sizes),
        in_specs=[pl.BlockSpec(memory_space=VMEM)] * (len(flat) + 1),
        out_specs=pl.BlockSpec(memory_space=pl.ANY),
        out_shape=jax.ShapeDtypeStruct((rows, cols), F32),
        scratch_shapes=[
            VMEM((block, 3 * count, width), BF16),
            VMEM((3 * count, cols), BF16),
            VMEM((stages, width, cols), F32),
            pltpu.SemaphoreType.DMA((stages,)),
        ],
        compiler_params=pltpu.CompilerParams(vmem_limit_bytes=12 << 20),
        name="update",
    )(*flat, covariance)


def body(features, cluster_ids, soft_weights, counts, centroids, covariance):
    peers = lax.axis_size("img")
    tiles = lax.axis_size("tile")
    clusters, width = centroids.shape
    images = features.shape[0]
    block = clusters // peers
    factor = float(width) / float(images * peers * tiles)

    def device(img, group, core):
        return (img * (tiles // 2) + group) * 2 + core

    everyone = [(i, g, c) for i in range(peers) for g in range(tiles // 2) for c in range(2)]

    def send(value, target):
        pairs = [(device(*d), device(*target(*d))) for d in everyone]
        return lax.ppermute(value, ("img", "tile"), pairs)

    def to_other(value):
        return send(value, lambda i, g, c: (i, g, 1 - c))

    def first(value, k):
        return send(value, lambda i, g, c: (i ^ k, g, c) if c == 0 else (i, g ^ k, c))

    def second(value, k):
        return send(value, lambda i, g, c: (i, g ^ k, c) if c == 0 else (i ^ k, g, c))

    own = aggregate(features, cluster_ids, soft_weights, counts, centroids)
    other = to_other(own)
    parts = pack(own, other, peers, block)
    received = [parts[0]]
    for k in range(1, peers):
        received.append(first(parts[k], k))
    middle = peers // 2
    gathered = [jnp.concatenate(received[:middle]), jnp.concatenate(received[middle:])]
    mine = [gathered]
    for k in range(1, peers):
        low = k & -k
        pieces = [jnp.concatenate(gathered)] if k == 1 else gathered
        arrived = []
        for n, piece in enumerate(pieces):
            if k != low and n == 0:
                arrived.append(second(mine[k - low][n], low))
            else:
                arrived.append(second(piece, k))
        mine.append(arrived)
    theirs = []
    for k in range(peers):
        pieces = mine[k] if k == peers - 1 else [jnp.concatenate(mine[k])]
        theirs.append([to_other(piece) for piece in pieces])
    return update(mine, theirs, covariance, factor)


def solution(mesh):
    return jax.shard_map(
        body,
        mesh=mesh,
        in_specs=(
            P(("img", "tile"), None, None),
            P(("img", "tile"), None, None),
            P(("img", "tile"), None, None),
            P(("img", "tile")),
            P(),
            P("img", "tile"),
        ),
        out_specs=P("img", "tile"),
        check_vma=False,
    )
```

```python
import functools

import jax
import jax.numpy as jnp
from jax import lax
from jax.experimental import pallas as pl
from jax.experimental.pallas import tpu as pltpu
from jax.sharding import PartitionSpec as P

VMEM = pltpu.VMEM
BF16 = jnp.bfloat16
F32 = jnp.float32


def aggregate_kernel(counts_in, ids_in, weights_in, centroids_in, features_in, rows, *scratch):
    counts, ids, weights, centroids, features, sems = scratch
    images, top, slots = ids.shape
    clusters = centroids.shape[0]
    small = [
        pltpu.make_async_copy(source, target, sems.at[n])
        for n, (source, target) in enumerate(
            [
                (counts_in, counts),
                (ids_in, ids),
                (weights_in, weights),
                (centroids_in, centroids),
            ]
        )
    ]
    large = [
        pltpu.make_async_copy(features_in.at[n], features.at[n], sems.at[len(small) + n])
        for n in range(images)
    ]
    for copy in small + large:
        copy.start()
    for copy in small:
        copy.wait()
    labels = lax.broadcasted_iota(jnp.int32, (clusters, slots), 0)
    position = lax.broadcasted_iota(jnp.int32, (top, slots), 1)
    assigned = []
    for image in range(images):
        valid_ids = jnp.where(position < counts[image], ids[image], -1)
        values = weights[image].astype(F32)
        assign = jnp.zeros((clusters, slots), F32)
        for slot in range(top):
            matched = valid_ids[slot : slot + 1] == labels
            assign = assign + jnp.where(matched, values[slot : slot + 1], 0.0)
        assign = assign.astype(BF16)
        weight_sum = jnp.sum(assign.astype(F32), axis=1, keepdims=True)
        assigned.append((assign, weight_sum * centroids[...].astype(F32)))
    for copy in large:
        copy.wait()
    for image, (assign, offset) in enumerate(assigned):
        residual = jnp.dot(assign, features[image], preferred_element_type=F32) - offset
        square = jnp.sum(residual * residual, axis=1, keepdims=True)
        rows[image] = residual / jnp.sqrt(square + 1e-06)


def aggregate(features, cluster_ids, soft_weights, counts, centroids):
    images, _, width = features.shape
    clusters = centroids.shape[0]
    return pl.pallas_call(
        aggregate_kernel,
        in_specs=[pl.BlockSpec(memory_space=pltpu.HBM)] * 5,
        out_specs=pl.BlockSpec(memory_space=VMEM),
        out_shape=VMEM((images, clusters, width), F32),
        scratch_shapes=[
            pltpu.SMEM(counts.shape, counts.dtype),
            VMEM(cluster_ids.shape, cluster_ids.dtype),
            VMEM(soft_weights.shape, soft_weights.dtype),
            VMEM(centroids.shape, centroids.dtype),
            VMEM(features.shape, features.dtype),
            pltpu.SemaphoreType.DMA((4 + images,)),
        ],
        compiler_params=pltpu.CompilerParams(vmem_limit_bytes=64000000),
        name="aggregate",
    )(counts, cluster_ids, soft_weights, centroids, features)


def pack_kernel(peers, block, own, other, *parts):
    core = lax.rem(lax.axis_index("tile"), 2)
    me = jnp.where(core == 0, lax.axis_index("img"), lax.axis_index("tile") // 2)
    images = own.shape[0]
    for step in range(peers):
        start = pl.multiple_of(lax.bitwise_xor(me, step) * block, block)
        parts[step][pl.ds(core * images, images)] = own[:, pl.ds(start, block)]
        parts[step][pl.ds((1 - core) * images, images)] = other[:, pl.ds(start, block)]


def pack(own, other, peers, block):
    images, _, width = own.shape
    return pl.pallas_call(
        functools.partial(pack_kernel, peers, block),
        in_specs=[pl.BlockSpec(memory_space=VMEM)] * 2,
        out_specs=[pl.BlockSpec(memory_space=VMEM)] * peers,
        out_shape=[jax.ShapeDtypeStruct((2 * images, block, width), F32)] * peers,
        compiler_params=pltpu.CompilerParams(vmem_limit_bytes=4 << 20),
        cost_estimate=pl.CostEstimate(flops=10**11, bytes_accessed=10**9, transcendentals=0),
        name="pack",
    )(own, other)


def split(value):
    high = value.astype(BF16)
    low = (value - high.astype(F32)).astype(BF16)
    return high, low


def update_kernel(peers, factor, stages, sizes, *refs):
    tree = [refs[sum(sizes[:n]) : sum(sizes[: n + 1])] for n in range(2 * peers)]
    mine, theirs = tree[:peers], tree[peers:]
    covariance, updated, left, right, stage, sems = refs[sum(sizes) :]
    core = lax.rem(lax.axis_index("tile"), 2)
    group = sum(ref.shape[0] for ref in mine[0])
    block, width = mine[0][0].shape[1:]
    part = group // peers
    count = group * peers
    half = block // 2

    def take(pieces, slot, cluster):
        size = pieces[0].shape[0]
        start = slot * part
        return pieces[start // size][start % size : start % size + part, cluster, :]

    def prepare_columns(col_refs, base):
        slots = [(j, t) for j in range(peers) for t in range(peers)]
        for k in range(half):
            pieces = [take(col_refs[t], j, base + k) for j, t in slots]
            high, low = split(jnp.concatenate(pieces, axis=0) * factor)
            columns = slice(k * width, (k + 1) * width)
            right[0 * count : 1 * count, columns] = high
            right[1 * count : 2 * count, columns] = low
            right[2 * count : 3 * count, columns] = high

    def prepare_rows(row_refs, clusters):
        for k in clusters:
            pieces = [ref[:, k, :] for refs_of in row_refs for ref in refs_of]
            high, low = split(jnp.concatenate(pieces, axis=0))
            left[k, 0 * count : 1 * count] = high
            left[k, 1 * count : 2 * count] = high
            left[k, 2 * count : 3 * count] = low

    lead = min(2, block)

    @pl.when(core == 0)
    def _():
        prepare_columns(theirs, 0)
        prepare_rows(mine, range(lead))

    @pl.when(core == 1)
    def _():
        prepare_columns(mine, half)
        prepare_rows(theirs, range(lead))

    def copy_out(step, slot):
        start = pl.multiple_of(step * width, width)
        return pltpu.make_async_copy(stage.at[slot], updated.at[pl.ds(start, width)], sems.at[slot])

    def row_step(step, carry):
        slot = lax.rem(step, stages)

        @pl.when(step >= stages)
        def _():
            copy_out(step - stages, slot).wait()

        product = lax.dot_general(
            left[step], right[...], (((0,), (0,)), ((), ())), preferred_element_type=F32
        )
        start = pl.multiple_of(step * width, width)
        stage[slot] = covariance[pl.ds(start, width)] + product
        copy_out(step, slot).start()
        return carry

    lax.fori_loop(0, lead, row_step, 0)

    @pl.when(core == 0)
    def _():
        prepare_rows(mine, range(lead, block))

    @pl.when(core == 1)
    def _():
        prepare_rows(theirs, range(lead, block))

    lax.fori_loop(lead, block, row_step, 0)
    for step in range(max(block - stages, 0), block):
        copy_out(step, step % stages).wait()


def update(mine, theirs, covariance, factor):
    peers = len(mine)
    sizes = [len(pieces) for pieces in mine + theirs]
    flat = [piece for pieces in mine + theirs for piece in pieces]
    block, width = flat[0].shape[1:]
    count = sum(piece.shape[0] for pieces in mine for piece in pieces)
    rows, cols = covariance.shape
    stages = 4
    return pl.pallas_call(
        functools.partial(update_kernel, peers, factor, stages, sizes),
        in_specs=[pl.BlockSpec(memory_space=VMEM)] * (len(flat) + 1),
        out_specs=pl.BlockSpec(memory_space=pl.ANY),
        out_shape=jax.ShapeDtypeStruct((rows, cols), F32),
        scratch_shapes=[
            VMEM((block, 3 * count, width), BF16),
            VMEM((3 * count, cols), BF16),
            VMEM((stages, width, cols), F32),
            pltpu.SemaphoreType.DMA((stages,)),
        ],
        compiler_params=pltpu.CompilerParams(vmem_limit_bytes=14 << 20),
        name="update",
    )(*flat, covariance)


def body(features, cluster_ids, soft_weights, counts, centroids, covariance):
    peers = lax.axis_size("img")
    tiles = lax.axis_size("tile")
    clusters, width = centroids.shape
    images = features.shape[0]
    block = clusters // peers
    factor = float(width) / float(images * peers * tiles)

    def device(img, group, core):
        return (img * (tiles // 2) + group) * 2 + core

    everyone = [(i, g, c) for i in range(peers) for g in range(tiles // 2) for c in range(2)]

    def send(value, target):
        pairs = [(device(*d), device(*target(*d))) for d in everyone]
        return lax.ppermute(value, ("img", "tile"), pairs)

    def to_other(value):
        return send(value, lambda i, g, c: (i, g, 1 - c))

    def first(value, k):
        return send(value, lambda i, g, c: (i ^ k, g, c) if c == 0 else (i, g ^ k, c))

    def second(value, k):
        return send(value, lambda i, g, c: (i, g ^ k, c) if c == 0 else (i ^ k, g, c))

    own = aggregate(features, cluster_ids, soft_weights, counts, centroids)
    other = to_other(own)
    parts = pack(own, other, peers, block)
    received = [parts[0]]
    for k in range(1, peers):
        received.append(first(parts[k], k))
    middle = peers // 2
    gathered = [jnp.concatenate(received[:middle]), jnp.concatenate(received[middle:])]
    mine = [gathered]
    for k in range(1, peers):
        low = k & -k
        pieces = [jnp.concatenate(gathered)] if k == 1 else gathered
        arrived = []
        for n, piece in enumerate(pieces):
            if k != low and n == 0:
                arrived.append(second(mine[k - low][n], low))
            else:
                arrived.append(second(piece, k))
        mine.append(arrived)
    theirs = []
    for k in range(peers):
        pieces = mine[k] if k == peers - 1 else [jnp.concatenate(mine[k])]
        theirs.append([to_other(piece) for piece in pieces])
    return update(mine, theirs, covariance, factor)


def solution(mesh):
    return jax.shard_map(
        body,
        mesh=mesh,
        in_specs=(
            P(("img", "tile"), None, None),
            P(("img", "tile"), None, None),
            P(("img", "tile"), None, None),
            P(("img", "tile")),
            P(),
            P("img", "tile"),
        ),
        out_specs=P("img", "tile"),
        check_vma=False,
    )
```
